32 devices in a mesh: feat: 8 (over z, y), ex: 4 (over x, core).
Axes of the slice: x: 2, y: 2, z: 4, core: 2. Of those that a mesh axis runs over, the one named last changes fastest.
Arguments:
- examples: bfloat16 [4096, 262144], P('ex', 'feat'), may hold values from -6 to 6
- weights: bfloat16 [262144], P('feat'), may hold values from -0.01171875 to 0.01171875
- labels: int32 [4096], P('ex'), may hold values from 0 to 1
- split: int32 [4096], P('ex'), may hold values 0 or 1
- val_weight: float32 [32, 4096], P(None, 'ex'), may hold values from 0.1 to 10
- strengths: float32 [256], replicated, may hold values from 0.05 to 1
- block_ids: int32 [262144], P('feat'), may hold values from 0 to 255
Outputs:
- solve: float32 [32, 262144], P(None, ('feat', 'ex'))
- hypergrad: float32 [32, 256], P(None, ('feat', 'ex'))
The draws below stay inside these ranges and needn't reach their ends.
All inputs are finite; a program needn't handle non-finite values. No bound on the sum of `split` on one device may be relied on, other than what follows from the above.
Results may differ from the reference program's by a relative error of at most 0.0029.
Values may be sent and summed in bfloat16 or wider, within the bound.
A program may use at most 128 MiB of HBM per device.

```python
import math
import jax
import jax.numpy as jnp
from jax import lax

F = 262144
NB = 256
R = 32
NEX = 4096


def set_ends(drawn, rng, smallest, high):
    longest = drawn.shape.index(max(drawn.shape))
    spots = []
    for shift in (0, 1):
        where = [jax.random.randint(jax.random.fold_in(rng, axis), (), 0, length) for axis, length in enumerate(drawn.shape)]
        where[longest] = (where[longest] + shift) % drawn.shape[longest]
        spots.append(tuple(where))
    return drawn.at[spots[0]].set(smallest).at[spots[1]].set(high)


def block_levels(key, shape, cuts, least, largest):
    def one(position, blocks):
        draws = jax.random.uniform(jax.random.fold_in(jax.random.fold_in(key, 6), position), (blocks,), jnp.float32, least / len(cuts), largest / len(cuts))
        return jnp.repeat(jnp.exp(draws), shape[position] // blocks).reshape((-1,) + (1,) * (len(shape) - position - 1))

    gain = one(*cuts[0])
    for cut in cuts[1:]:
        gain = gain * one(*cut)
    return gain


def gaussian(key, extent, scale, reach, shards=(), kind=jnp.bfloat16):
    array = scale * jax.random.normal(key, extent, jnp.float32)
    if shards:
        array = array * block_levels(key, extent, shards, -0.22, 0.18)
    return jnp.clip(array, -reach, reach).astype(kind)


def setup_inputs(seed: int = 0) -> dict:
    seeds = jax.random.split(jax.random.key(seed), 8)
    examples = gaussian(seeds[0], (NEX, F), 1.0, 6.0, ((0, 4), (1, 8)))
    weights = gaussian(seeds[1], (F,), F ** -0.5, 0.01171875, ((0, 8),))
    labels = set_ends(jax.random.randint(seeds[2], (NEX,), 0, 2), jax.random.fold_in(seeds[2], 1), 0, 1).astype(jnp.int32)
    split = set_ends((jax.random.randint(seeds[3], (NEX,), 0, 4) < 3).astype(jnp.int32), jax.random.fold_in(seeds[3], 1), 0, 1)
    val_weight = jnp.clip(jnp.exp(math.log(10.0) - 4.6051702 * jax.random.uniform(seeds[4], (R, NEX), jnp.float32) ** block_levels(seeds[4], (R, NEX), ((1, 4),), -0.2, 0.2)), 0.1, 10.0)
    strengths = jnp.clip(jnp.exp(jax.random.uniform(seeds[5], (NB,), jnp.float32, math.log(0.05), math.log(1.0))), 0.05, 1.0)
    block_ids = set_ends(jax.random.randint(seeds[6], (F,), 0, NB), jax.random.fold_in(seeds[6], 1), 0, NB - 1).astype(jnp.int32)
    return {"examples": examples, "weights": weights, "labels": labels, "split": split, "val_weight": val_weight, "strengths": strengths, "block_ids": block_ids}


def reference(examples, weights, labels, split, val_weight, strengths, block_ids):
    margin = jnp.dot(examples, weights, preferred_element_type=jnp.float32)
    prob = 1.0 / (1.0 + jnp.exp(-margin))
    train = split.astype(jnp.float32)
    curvew = train * prob * (1.0 - prob)
    err = (1.0 - train) * (prob - labels.astype(jnp.float32))
    gradw = (val_weight * err[None, :] / jnp.sqrt(jnp.float32(NEX))).astype(jnp.bfloat16)
    rhs = jnp.dot(gradw, examples, preferred_element_type=jnp.float32)
    lamf = strengths[block_ids]

    def apply_hessian(direc):
        dlow = direc.astype(jnp.bfloat16)
        tang = jnp.dot(dlow, examples.T, preferred_element_type=jnp.float32)
        wtang = (curvew[None, :] * tang).astype(jnp.bfloat16)
        prod = jnp.dot(wtang, examples, preferred_element_type=jnp.float32)
        return prod / jnp.float32(NEX) + lamf[None, :] * direc
    solve = jnp.zeros_like(rhs)
    resid = rhs
    direc = rhs
    norm_now = lax.optimization_barrier(jnp.sum(resid * resid, axis=1))
    for step in range(2):
        image = apply_hessian(direc)
        curv = lax.optimization_barrier(jnp.sum(direc * image, axis=1))
        alpha = norm_now / curv
        solve = solve + alpha[:, None] * direc
        resid = resid - alpha[:, None] * image
        if step == 0:
            norm_next = lax.optimization_barrier(jnp.sum(resid * resid, axis=1))
            direc = resid + (norm_next / norm_now)[:, None] * direc
            norm_now = norm_next
    product = solve * weights.astype(jnp.float32)[None, :]
    sums = jax.ops.segment_sum(product.T, block_ids, num_segments=NB).T
    return (solve, -strengths[None, :] * sums)
```

```python
import functools
import math

import jax
import jax.numpy as jnp
from jax import lax
from jax.experimental import pallas as pl
from jax.experimental.pallas import tpu as pltpu
from jax.sharding import PartitionSpec as P

MESH = pl.DeviceIdType.MESH
VMEM = pl.BlockSpec(memory_space=pltpu.VMEM)
ANY = pl.BlockSpec(memory_space=pl.ANY)
LANES = 128
LAG_SUM, LAG_LOW, LAG_TANG = 1, 3, 4
RING_BYTES = 32 * 2**20


def address(axis, pos):
    if axis == "feat":
        return (pos, lax.axis_index("ex"))
    return (lax.axis_index("feat"), pos)


def flip(pos, mask):
    return pos + mask * (1 - 2 * lax.rem(lax.div(pos, mask), 2))


def fold(x):
    total = x[:, :LANES]
    for at in range(LANES, x.shape[1], LANES):
        total = total + x[:, at : at + LANES]
    return total


def pick(packet, lane):
    lanes = lax.broadcasted_iota(jnp.int32, packet.shape, 1)
    return jnp.sum(jnp.where(lanes == lane, packet, 0.0), axis=1, keepdims=True)


def packed(columns, rows):
    lanes = lax.broadcasted_iota(jnp.int32, (rows, LANES), 1)
    out = jnp.zeros((rows, LANES), jnp.float32)
    for lane, column in enumerate(columns):
        out = jnp.where(lanes == lane, column, out)
    return out


def split_in(x, pieces):
    parts = []
    for _ in range(pieces):
        part = x.astype(jnp.bfloat16)
        parts.append(part)
        x = x - part.astype(jnp.float32)
    return parts


def one_hot(ids, blocks):
    rows = lax.broadcasted_iota(jnp.int32, (blocks, ids.shape[1]), 0)
    return (rows == ids).astype(jnp.float32).astype(jnp.bfloat16)


def kernel(
    dims,
    x_hbm,
    w_ref,
    ids_ref,
    labels_ref,
    split_ref,
    vw_ref,
    strengths_ref,
    solve_ref,
    hyper_ref,
    ring,
    margin,
    margins,
    lam,
    curvew,
    left,
    keep,
    out_a,
    in_a,
    out_b,
    in_b,
    low,
    rhs,
    tang,
    parts,
    gathered,
    sums,
    coef,
    packets,
    grouped,
    groups,
    group_parts,
    own_groups,
    own_parts,
    own_strengths,
    ring_sem,
    pair_sem,
    feat_sem,
    ex_sem,
):
    nf, ne, n, width, rows, blocks, share, size, chunks, slots = dims
    total = n * ne
    groups_n = n // LANES
    owners = min(nf, groups_n)
    per = groups_n // owners
    nb_feat = blocks // nf
    nb_own = nb_feat // ne
    me_f = lax.axis_index("feat")
    me_e = lax.axis_index("ex")
    core = lax.rem(me_e, 2)
    side = lax.div(me_e, 2)
    half = 2 * size

    barrier = pltpu.get_barrier_semaphore()
    for axis, me, count in (("feat", me_f, nf), ("ex", me_e, ne)):
        for k in range(1, count):
            pl.semaphore_signal(
                barrier, inc=1, device_id=address(axis, lax.rem(me + k, count)), device_id_type=MESH
            )

    def load(turn):
        chunk = lax.rem(turn, chunks)
        slot = lax.rem(turn, slots)
        copies = []
        for h in range(2):
            for x in range(2):
                at = pl.multiple_of((h + 2 * x) * share + chunk * size, LANES)
                copies.append(
                    pltpu.make_async_copy(
                        x_hbm.at[:, pl.ds(at, size)],
                        ring.at[slot, :, pl.ds(h * half + x * size, size)],
                        ring_sem.at[slot, 2 * h + x],
                    )
                )
        return copies

    def begin(turn):
        for copy in load(turn):
            copy.start()

    def arrived(turn):
        for copy in load(turn):
            copy.wait()

    def refill(turn):
        @pl.when(turn + slots < 3 * chunks)
        def _():
            begin(turn + slots)

    for turn in range(min(slots, 3 * chunks)):
        begin(turn)

    def columns(ref, chunk, h, x):
        at = pl.multiple_of((h + 2 * x) * share + chunk * size, LANES)
        return ref[:, pl.ds(at, size)]

    levels = jnp.concatenate(
        split_in(strengths_ref[...], 3) + [jnp.zeros((5, blocks), jnp.bfloat16)], axis=0
    )
    own_strengths[...] = jnp.transpose(jnp.broadcast_to(strengths_ref[...], (8, blocks)))
    margin[...] = jnp.zeros_like(margin)

    @pl.loop(0, chunks)
    def _(i):
        arrived(i)
        slot = lax.rem(i, slots)
        w = jnp.concatenate([columns(w_ref, i, h, x) for h in range(2) for x in range(2)], axis=1)
        part = lax.dot_general(
            w.astype(jnp.bfloat16), ring[slot], (((1,), (1,)), ((), ())), preferred_element_type=jnp.float32
        )
        for g in range(groups_n):
            margin[g : g + 1, :] += part[:, g * LANES : (g + 1) * LANES]
        refill(i)
        ids = jnp.concatenate([columns(ids_ref, i, core, x) for x in range(2)], axis=1)
        found = jnp.dot(levels, one_hot(ids, blocks), preferred_element_type=jnp.float32)
        lam[i] = found[0:1] + found[1:2] + found[2:3]

    pl.semaphore_wait(barrier, nf - 1 + ne - 1)

    def remote(src, dst, sems, axis, peer):
        return pltpu.make_async_remote_copy(
            src_ref=src,
            dst_ref=dst,
            send_sem=sems[0],
            recv_sem=sems[1],
            device_id=address(axis, peer),
            device_id_type=MESH,
        )

    def feat_copies(src, dst, kind):
        return [
            remote(src(lax.rem(me_f + k, nf)), dst(k), [feat_sem.at[kind, d, k] for d in range(2)], "feat", lax.rem(me_f + k, nf))
            for k in range(1, nf)
        ]

    def ex_copies(src, dst, kind):
        return [
            remote(src(lax.rem(me_e + k, ne)), dst(k), [ex_sem.at[kind, d, k] for d in range(2)], "ex", lax.rem(me_e + k, ne))
            for k in range(1, ne)
        ]

    def launch(copies):
        for copy in copies:
            copy.start()
        return copies

    waiting = []

    def receive(copies):
        for copy in copies:
            copy.wait_recv()
        waiting.extend(copies)

    receive(launch(feat_copies(lambda peer: margin, lambda k: margins.at[k], 0)))
    whole = margin[...]
    for k in range(1, nf):
        whole = whole + margins[k]
    prob = 1.0 / (1.0 + jnp.exp(-whole))
    train = split_ref[...].astype(jnp.float32)
    curvew[...] = train * prob * (1.0 - prob)
    err = (1.0 - train) * (prob - labels_ref[...].astype(jnp.float32))
    root = jnp.float32(math.sqrt(total))
    for g in range(groups_n):
        at = slice(g * LANES, (g + 1) * LANES)
        left[:, at] = (vw_ref[:, at] * err[g : g + 1] / root).astype(jnp.bfloat16)

    def pair_copy(phase, kind, chunk):
        src, dst, mask = (
            (out_a.at[phase, chunk], in_a.at[phase, chunk], 1),
            (out_b.at[phase, chunk], in_b.at[phase, chunk], 2),
            (low.at[phase, chunk, core], low.at[phase, chunk, core], 1),
        )[kind]
        return remote(src, dst, [pair_sem.at[phase, kind, d, chunk] for d in range(2)], "ex", flip(me_e, mask))

    def product(phase, finish):
        tang[phase] = jnp.zeros_like(tang[phase])
        base = (phase + 1) * chunks

        @pl.loop(0, chunks + LAG_TANG)
        def _(i):
            @pl.when((i >= LAG_LOW) & (i < chunks + LAG_LOW))
            def _():
                chunk = i - LAG_LOW
                pair_copy(phase, 1, chunk).wait_recv()
                value = finish(chunk, keep[chunk] + in_b[phase, chunk].astype(jnp.float32))
                low[phase, chunk, core] = value.astype(jnp.bfloat16)
                pair_copy(phase, 2, chunk).start()

            @pl.when((i >= LAG_SUM) & (i < chunks + LAG_SUM))
            def _():
                chunk = i - LAG_SUM
                pair_copy(phase, 0, chunk).wait_recv()
                value = keep[chunk] + in_a[phase, chunk].astype(jnp.float32)
                keep[chunk] = value
                out_b[phase, chunk] = value.astype(jnp.bfloat16)
                pair_copy(phase, 1, chunk).start()

            @pl.when(i < chunks)
            def _():
                arrived(base + i)
                slot = lax.rem(base + i, slots)
                away = ring[slot, :, pl.ds(pl.multiple_of((1 - core) * half, LANES), half)]
                out_a[phase, i] = jnp.dot(left[...], away, preferred_element_type=jnp.float32).astype(jnp.bfloat16)
                pair_copy(phase, 0, i).start()
                mine = ring[slot, :, pl.ds(pl.multiple_of(core * half, LANES), half)]
                keep[i] = jnp.dot(left[...], mine, preferred_element_type=jnp.float32)

            @pl.when(i >= LAG_TANG)
            def _():
                chunk = i - LAG_TANG
                slot = lax.rem(base + chunk, slots)
                pair_copy(phase, 2, chunk).wait_recv()
                direc = jnp.concatenate([low[phase, chunk, 0], low[phase, chunk, 1]], axis=1)
                part = lax.dot_general(
                    direc, ring[slot], (((1,), (1,)), ((), ())), preferred_element_type=jnp.float32
                )
                for g in range(groups_n):
                    tang[phase, g] += part[:, g * LANES : (g + 1) * LANES]
                refill(base + chunk)

    def scattered(phase):
        peers = [lax.rem(me_f + k, nf) for k in range(1, nf)]
        copies = feat_copies(
            lambda peer: tang.at[phase, pl.ds(lax.rem(peer, owners) * per, per)], lambda k: parts.at[phase, k], 1 + phase
        )
        if owners == nf:
            receive(launch(copies))
        else:
            for peer, copy in zip(peers, copies):
                pl.when(peer < owners)(copy.start)

            @pl.when(me_f < owners)
            def _():
                for copy in copies:
                    copy.wait_recv()

            for peer, copy in zip(peers, copies):
                pl.when(peer < owners)(copy.wait_send)
        value = tang[phase, pl.ds(lax.rem(me_f, owners) * per, per)]
        for k in range(1, nf):
            value = value + parts[phase, k]
        if owners == nf:
            return value
        return jnp.where(me_f < owners, value, 0.0)

    def own_part(ref, chunk):
        return ref[chunk, :, pl.ds(pl.multiple_of(side * size, LANES), size)]

    sums[...] = jnp.zeros_like(sums)

    def first_low(chunk, value):
        rhs[chunk] = value
        own = own_part(rhs, chunk)
        square = own * own
        sums[0] += fold(square)
        sums[1] += fold(square * own_part(lam, chunk))
        return value

    product(0, first_low)

    first_row = lax.rem(me_f, owners) * per

    def weighted(value, other):
        out = jnp.zeros((rows, LANES), jnp.float32)
        for t in range(per):
            out = out + curvew[pl.ds(first_row + t, 1), :] * value[t] * other[t]
        return jnp.sum(out, axis=1, keepdims=True)

    mine = scattered(0)
    gathered[me_f, 0:per] = mine
    gathered[me_f, per] = packed(
        [
            jnp.sum(sums[0], axis=1, keepdims=True),
            jnp.sum(sums[1], axis=1, keepdims=True),
            weighted(mine, mine),
        ],
        rows,
    )
    receive(launch(feat_copies(lambda peer: gathered.at[me_f], lambda k: gathered.at[me_f], 3)))
    packet = gathered[0, per]
    for f in range(1, nf):
        packet = packet + gathered[f, per]
    packets[0, 0] = packet
    shared = launch(ex_copies(lambda peer: packets.at[0, 0], lambda k: packets.at[0, k], 0))
    waiting.extend(shared)
    for g in range(groups_n):
        left[:, g * LANES : (g + 1) * LANES] = (curvew[g : g + 1] * gathered[g // per, g % per]).astype(jnp.bfloat16)

    sums[...] = jnp.zeros_like(sums)
    grouped[...] = jnp.zeros_like(grouped)

    def second_low(chunk, value):
        @pl.when(chunk == 0)
        def _():
            for copy in shared:
                copy.wait_recv()
            packet = packets[0, 0]
            for k in range(1, ne):
                packet = packet + packets[0, k]
            norm, damp, along = (pick(packet, lane) for lane in range(3))
            alpha = norm / (along / total + damp)
            for at, column in enumerate((alpha, norm, damp, along)):
                coef[at] = jnp.broadcast_to(column, (rows, LANES))

        base = rhs[chunk]
        value = base - coef[0, :, 0:1] * (value / total + lam[chunk] * base)
        keep[chunk] = value
        own = own_part(keep, chunk)
        before = own_part(rhs, chunk)
        scaled = own_part(lam, chunk) * own
        sums[0] += fold(own * own)
        sums[1] += fold(scaled * own)
        sums[2] += fold(scaled * before)
        solve_ref[:, pl.ds(pl.multiple_of(chunk * size, LANES), size)] = own
        at = pl.multiple_of(me_e * share + chunk * size, LANES)
        w = w_ref[:, pl.ds(at, size)]
        pieces = jnp.concatenate(split_in(before * w, 2) + split_in(own * w, 2), axis=0)
        grouped[...] += lax.dot_general(
            one_hot(ids_ref[:, pl.ds(at, size)], blocks),
            pieces,
            (((1,), (1,)), ((), ())),
            preferred_element_type=jnp.float32,
        )
        return value

    product(1, second_low)

    for f in range(nf):
        groups[f] = grouped[f * nb_feat : (f + 1) * nb_feat, :]
    sent = launch(feat_copies(lambda peer: groups.at[peer], lambda k: group_parts.at[k], 4))
    turned = scattered(1)
    receive(sent)
    owned = groups[me_f]
    for k in range(1, nf):
        owned = owned + group_parts[k]
    for e in range(ne):
        own_groups[e] = owned[e * nb_own : (e + 1) * nb_own, :]
    held = gathered[me_f, 0:per]
    packets[1, 0] = packed(
        [jnp.sum(sums[at], axis=1, keepdims=True) for at in range(3)]
        + [weighted(turned, turned), weighted(turned, held)],
        rows,
    )
    receive(
        launch(
            ex_copies(lambda peer: packets.at[1, 0], lambda k: packets.at[1, k], 1)
            + ex_copies(lambda peer: own_groups.at[peer], lambda k: own_parts.at[k], 2)
        )
    )
    packet = packets[1, 0]
    for k in range(1, ne):
        packet = packet + packets[1, k]
    packets[2, 0] = packet
    receive(launch(feat_copies(lambda peer: packets.at[2, 0], lambda k: parts.at[2, k, 0], 5)))
    for k in range(1, nf):
        packet = packet + parts[2, k, 0]

    norm_next, damp_next, damp_cross, curved_next, curved_cross = (pick(packet, lane) for lane in range(5))
    alpha, norm, damp, along = (coef[at, :, 0:1] for at in range(4))
    beta = norm_next / norm
    curved = curved_next + 2.0 * beta * curved_cross + beta * beta * along
    damped = damp_next + 2.0 * beta * damp_cross + beta * beta * damp
    step = norm_next / (curved / total + damped)
    first = alpha + step * beta

    @pl.loop(0, chunks)
    def _(i):
        at = pl.ds(pl.multiple_of(i * size, LANES), size)
        solve_ref[:, at] = first * own_part(rhs, i) + step * solve_ref[:, at]

    mine = own_groups[me_e]
    for k in range(1, ne):
        mine = mine + own_parts[k]
    first_block = (me_f * ne + me_e) * nb_own
    scale = own_strengths[pl.ds(first_block, nb_own), 0:1]
    mine = jnp.concatenate([-scale * mine, jnp.zeros((8 * pl.cdiv(nb_own, 8) - nb_own, LANES), jnp.float32)], axis=0) if nb_own % 8 else -scale * mine
    mine = jnp.transpose(mine)[:, :nb_own]
    hyper_ref[...] = first * (mine[:rows] + mine[rows : 2 * rows]) + step * (
        mine[2 * rows : 3 * rows] + mine[3 * rows : 4 * rows]
    )

    for copy in waiting:
        copy.wait_send()

    @pl.loop(0, chunks)
    def _(i):
        for phase in range(2):
            for kind in range(3):
                pair_copy(phase, kind, i).wait_send()


def shards(examples, weights, labels, split, val_weight, strengths, block_ids):
    ne = lax.axis_size("ex")
    nf = lax.axis_size("feat")
    n, width = examples.shape
    rows = val_weight.shape[0]
    blocks = strengths.shape[0]
    share = width // ne
    size = LANES
    while size < 512 and share % (2 * size) == 0:
        size *= 2
    chunks = share // size
    slots = max(LAG_TANG + 2, RING_BYTES // (2 * n * ne * size))
    groups_n = n // LANES
    per = groups_n // min(nf, groups_n)
    nb_feat = blocks // nf
    nb_own = nb_feat // ne
    dims = (nf, ne, n, width, rows, blocks, share, size, chunks, slots)
    half = 2 * size
    f32, bf16 = jnp.float32, jnp.bfloat16
    return pl.pallas_call(
        functools.partial(kernel, dims),
        out_shape=(
            jax.ShapeDtypeStruct((rows, share), f32),
            jax.ShapeDtypeStruct((rows, nb_own), f32),
        ),
        in_specs=[ANY] + [VMEM] * 6,
        out_specs=(VMEM, VMEM),
        scratch_shapes=[
            pltpu.VMEM((slots, n, 2 * half), bf16),
            pltpu.VMEM((groups_n, LANES), f32),
            pltpu.VMEM((nf, groups_n, LANES), f32),
            pltpu.VMEM((chunks, 1, half), f32),
            pltpu.VMEM((groups_n, LANES), f32),
            pltpu.VMEM((rows, n), bf16),
            pltpu.VMEM((chunks, rows, half), f32),
            pltpu.VMEM((2, chunks, rows, half), bf16),
            pltpu.VMEM((2, chunks, rows, half), bf16),
            pltpu.VMEM((2, chunks, rows, half), bf16),
            pltpu.VMEM((2, chunks, rows, half), bf16),
            pltpu.VMEM((2, chunks, 2, rows, half), bf16),
            pltpu.VMEM((chunks, rows, half), f32),
            pltpu.VMEM((2, groups_n, rows, LANES), f32),
            pltpu.VMEM((3, nf, per, rows, LANES), f32),
            pltpu.VMEM((nf, per + 1, rows, LANES), f32),
            pltpu.VMEM((3, rows, LANES), f32),
            pltpu.VMEM((4, rows, LANES), f32),
            pltpu.VMEM((3, ne, rows, LANES), f32),
            pltpu.VMEM((blocks, 4 * rows), f32),
            pltpu.VMEM((nf, nb_feat, 4 * rows), f32),
            pltpu.VMEM((nf, nb_feat, 4 * rows), f32),
            pltpu.VMEM((ne, nb_own, 4 * rows), f32),
            pltpu.VMEM((ne, nb_own, 4 * rows), f32),
            pltpu.VMEM((blocks, 8), f32),
            pltpu.SemaphoreType.DMA((slots, 4)),
            pltpu.SemaphoreType.DMA((2, 3, 2, chunks)),
            pltpu.SemaphoreType.DMA((6, 2, nf)),
            pltpu.SemaphoreType.DMA((3, 2, ne)),
        ],
        compiler_params=pltpu.CompilerParams(
            collective_id=0, has_side_effects=True, vmem_limit_bytes=60 * 2**20
        ),
    )(
        examples,
        weights.astype(f32).reshape(1, width),
        block_ids.reshape(1, width),
        labels.reshape(groups_n, LANES),
        split.reshape(groups_n, LANES),
        val_weight,
        strengths.reshape(1, blocks),
    )


def solution(mesh):
    placed = (P("ex", "feat"), P("feat"), P("ex"), P("ex"), P(None, "ex"), P(), P("feat"))
    return jax.shard_map(
        shards,
        mesh=mesh,
        in_specs=placed,
        out_specs=(P(None, ("feat", "ex")), P(None, ("feat", "ex"))),
        check_vma=False,
    )
```

```python
import functools
import math

import jax
import jax.numpy as jnp
from jax import lax
from jax.experimental import pallas as pl
from jax.experimental.pallas import tpu as pltpu
from jax.sharding import PartitionSpec as P

MESH = pl.DeviceIdType.MESH
VMEM = pl.BlockSpec(memory_space=pltpu.VMEM)
ANY = pl.BlockSpec(memory_space=pl.ANY)
LANES = 128
LAG_SUM, LAG_LOW, LAG_TANG = 1, 4, 5
RING_BYTES = 32 * 2**20


def address(axis, pos):
    if axis == "feat":
        return (pos, lax.axis_index("ex"))
    return (lax.axis_index("feat"), pos)


def flip(pos, mask):
    return pos + mask * (1 - 2 * lax.rem(lax.div(pos, mask), 2))


def fold(x):
    total = x[:, :LANES]
    for at in range(LANES, x.shape[1], LANES):
        total = total + x[:, at : at + LANES]
    return total


def packed(columns):
    rows = columns[0].shape[0]
    lanes = lax.broadcasted_iota(jnp.int32, (rows, LANES), 1)
    out = jnp.zeros((rows, LANES), jnp.float32)
    for lane, column in enumerate(columns):
        out = jnp.where(lanes == lane, column, out)
    out = jnp.transpose(out)[:8]
    return jnp.concatenate([out, jnp.zeros((8, LANES - rows), jnp.float32)], axis=1)


def split_in(x, pieces):
    parts = []
    for _ in range(pieces):
        part = x.astype(jnp.bfloat16)
        parts.append(part)
        x = x - part.astype(jnp.float32)
    return parts


def one_hot(ids, blocks):
    rows = lax.broadcasted_iota(jnp.int32, (blocks, ids.shape[1]), 0)
    return (rows == ids).astype(jnp.float32).astype(jnp.bfloat16)


def kernel(
    dims,
    x_hbm,
    w_ref,
    ids_ref,
    labels_ref,
    split_ref,
    vw_ref,
    strengths_ref,
    base_hbm,
    resid_hbm,
    coef_ref,
    hyper_ref,
    ring,
    turned_x,
    weights,
    margin,
    margins,
    lam,
    curvew,
    left,
    out_a,
    in_a,
    out_b,
    in_b,
    low,
    rhs,
    tang,
    parts,
    held,
    gathered,
    sums,
    alpha,
    packets,
    feat_packets,
    grouped,
    groups,
    group_parts,
    own_groups,
    own_parts,
    own_strengths,
    resid,
    ring_sem,
    out_sem,
    pair_sem,
    feat_sem,
    ex_sem,
):
    nf, ne, n, width, rows, blocks, share, size, chunks, slots = dims
    total = n * ne
    groups_n = n // LANES
    owners = min(nf, groups_n)
    per = groups_n // owners
    nb_feat = blocks // nf
    nb_own = nb_feat // ne
    me_f = lax.axis_index("feat")
    me_e = lax.axis_index("ex")
    core = lax.rem(me_e, 2)
    side = lax.div(me_e, 2)
    half = 2 * size

    barrier = pltpu.get_barrier_semaphore()
    for axis, me, count in (("feat", me_f, nf), ("ex", me_e, ne)):
        for k in range(1, count):
            pl.semaphore_signal(
                barrier, inc=1, device_id=address(axis, lax.rem(me + k, count)), device_id_type=MESH
            )

    def load(turn):
        chunk = lax.rem(turn, chunks)
        slot = lax.rem(turn, slots)
        copies = []
        for h in range(2):
            for x in range(2):
                at = pl.multiple_of((h + 2 * x) * share + chunk * size, LANES)
                copies.append(
                    pltpu.make_async_copy(
                        x_hbm.at[:, pl.ds(at, size)],
                        ring.at[slot, :, pl.ds(h * half + x * size, size)],
                        ring_sem.at[slot, 2 * h + x],
                    )
                )
        return copies

    def begin(turn):
        for copy in load(turn):
            copy.start()

    def arrived(turn):
        for copy in load(turn):
            copy.wait()

    def refill(turn):
        @pl.when(turn + slots < 3 * chunks)
        def _():
            begin(turn + slots)

    for turn in range(min(slots, 3 * chunks)):
        begin(turn)

    def columns(ref, chunk, h, x):
        at = pl.multiple_of((h + 2 * x) * share + chunk * size, LANES)
        return ref[:, pl.ds(at, size)]

    levels = jnp.concatenate(
        split_in(strengths_ref[...], 3) + [jnp.zeros((5, blocks), jnp.bfloat16)], axis=0
    )
    own_strengths[...] = jnp.transpose(jnp.broadcast_to(strengths_ref[...], (8, blocks)))
    margin[...] = jnp.zeros_like(margin)
    weights[...] = w_ref[...].astype(jnp.float32)

    def weight_row(start):
        row = lax.div(start, LANES)
        return jnp.concatenate([weights[pl.ds(row + t, 1), :] for t in range(size // LANES)], axis=1)

    @pl.loop(0, chunks)
    def _(i):
        arrived(i)
        slot = lax.rem(i, slots)
        w = jnp.concatenate([weight_row((h + 2 * x) * share + i * size) for h in range(2) for x in range(2)], axis=1)
        part = lax.dot_general(
            w.astype(jnp.bfloat16), ring[slot], (((1,), (1,)), ((), ())), preferred_element_type=jnp.float32
        )
        for g in range(groups_n):
            margin[g : g + 1, :] += part[:, g * LANES : (g + 1) * LANES]
        refill(i)
        ids = jnp.concatenate([columns(ids_ref, i, core, x) for x in range(2)], axis=1)
        found = jnp.dot(levels, one_hot(ids, blocks), preferred_element_type=jnp.float32)
        lam[i] = found[0:1] + found[1:2] + found[2:3]

    pl.semaphore_wait(barrier, nf - 1 + ne - 1)

    def remote(src, dst, sems, axis, peer):
        return pltpu.make_async_remote_copy(
            src_ref=src,
            dst_ref=dst,
            send_sem=sems[0],
            recv_sem=sems[1],
            device_id=address(axis, peer),
            device_id_type=MESH,
        )

    def feat_copies(src, dst, kind):
        return [
            remote(src(lax.rem(me_f + k, nf)), dst(k), [feat_sem.at[kind, d, k] for d in range(2)], "feat", lax.rem(me_f + k, nf))
            for k in range(1, nf)
        ]

    def ex_copies(src, dst, kind):
        return [
            remote(src(lax.rem(me_e + k, ne)), dst(k), [ex_sem.at[kind, d, k] for d in range(2)], "ex", lax.rem(me_e + k, ne))
            for k in range(1, ne)
        ]

    def launch(copies):
        for copy in copies:
            copy.start()
        return copies

    waiting = []

    def receive(copies):
        for copy in copies:
            copy.wait_recv()
        waiting.extend(copies)

    receive(launch(feat_copies(lambda peer: margin, lambda k: margins.at[k], 0)))
    whole = margin[...]
    for k in range(1, nf):
        whole = whole + margins[k]
    prob = 1.0 / (1.0 + jnp.exp(-whole))
    train = split_ref[...].astype(jnp.float32)
    curvew[...] = train * prob * (1.0 - prob)
    err = (1.0 - train) * (prob - labels_ref[...].astype(jnp.float32))
    root = jnp.float32(math.sqrt(total))
    for g in range(groups_n):
        at = slice(g * LANES, (g + 1) * LANES)
        left[:, at] = (vw_ref[:, at] * err[g : g + 1] / root).astype(jnp.bfloat16)

    def pair_copy(phase, kind, chunk):
        src, dst, mask = (
            (out_a.at[phase, chunk], in_a.at[phase, chunk], 1),
            (out_b.at[phase, chunk], in_b.at[phase, chunk], 2),
            (low.at[phase, chunk, core], low.at[phase, chunk, core], 1),
        )[kind]
        return remote(src, dst, [pair_sem.at[phase, kind, d, chunk] for d in range(2)], "ex", flip(me_e, mask))

    def product(phase, finish, account):
        tang[phase] = jnp.zeros_like(tang[phase])
        base = (phase + 1) * chunks
        keep = (rhs, resid)[phase]

        def low_step(i):
            chunk = i - LAG_LOW
            pair_copy(phase, 1, chunk).wait_recv()
            value = finish(chunk, keep[chunk] + in_b[phase, chunk].astype(jnp.float32))
            low[phase, chunk, core] = value.astype(jnp.bfloat16)
            pair_copy(phase, 2, chunk).start()

        def sum_step(i):
            chunk = i - LAG_SUM
            pair_copy(phase, 0, chunk).wait_recv()
            value = keep[chunk] + in_a[phase, chunk].astype(jnp.float32)
            keep[chunk] = value
            out_b[phase, chunk] = value.astype(jnp.bfloat16)
            pair_copy(phase, 1, chunk).start()

        def matmuls(i, first, second):
            if first:
                arrived(base + i)
                slot = lax.rem(base + i, slots)
                away = ring[slot, :, pl.ds(pl.multiple_of((1 - core) * half, LANES), half)]
                out_a[phase, i] = jnp.dot(left[...], away, preferred_element_type=jnp.float32).astype(jnp.bfloat16)
                pair_copy(phase, 0, i).start()
            if second:
                chunk = i - LAG_TANG
                held_slot = lax.rem(base + chunk, slots)
                pair_copy(phase, 2, chunk).wait_recv()
                account(chunk)
                turned_x[...] = jnp.transpose(ring[held_slot])
            if first:
                mine = ring[slot, :, pl.ds(pl.multiple_of(core * half, LANES), half)]
                keep[i] = jnp.dot(left[...], mine, preferred_element_type=jnp.float32)
            if second:
                direc = jnp.concatenate([low[phase, chunk, 0], low[phase, chunk, 1]], axis=1)
                part = jnp.dot(direc, turned_x[...], preferred_element_type=jnp.float32)
                for g in range(groups_n):
                    tang[phase, g] += part[:, g * LANES : (g + 1) * LANES]
                refill(base + chunk)

        ramp = min(LAG_TANG, chunks)

        @pl.loop(0, ramp)
        def _(i):
            pl.when((i >= LAG_LOW) & (i < chunks + LAG_LOW))(lambda: low_step(i))
            pl.when((i >= LAG_SUM) & (i < chunks + LAG_SUM))(lambda: sum_step(i))
            matmuls(i, True, False)

        @pl.loop(ramp, chunks)
        def _(i):
            low_step(i)
            sum_step(i)
            matmuls(i, True, True)

        @pl.loop(chunks, chunks + LAG_TANG)
        def _(i):
            pl.when((i >= LAG_LOW) & (i < chunks + LAG_LOW))(lambda: low_step(i))
            pl.when((i >= LAG_SUM) & (i < chunks + LAG_SUM))(lambda: sum_step(i))
            pl.when(i >= LAG_TANG)(lambda: matmuls(i, False, True))

    def scattered(phase):
        peers = [lax.rem(me_f + k, nf) for k in range(1, nf)]
        copies = feat_copies(
            lambda peer: tang.at[phase, pl.ds(lax.rem(peer, owners) * per, per)], lambda k: parts.at[phase, k], 1 + phase
        )
        if owners == nf:
            receive(launch(copies))
        else:
            for peer, copy in zip(peers, copies):
                pl.when(peer < owners)(copy.start)

            @pl.when(me_f < owners)
            def _():
                for copy in copies:
                    copy.wait_recv()

            for peer, copy in zip(peers, copies):
                pl.when(peer < owners)(copy.wait_send)
        value = tang[phase, pl.ds(lax.rem(me_f, owners) * per, per)]
        for k in range(1, nf):
            value = value + parts[phase, k]
        if owners == nf:
            return value
        return jnp.where(me_f < owners, value, 0.0)

    def own_part(ref, chunk):
        return ref[chunk, :, pl.ds(pl.multiple_of(side * size, LANES), size)]

    def out_copy(phase, chunk):
        src, dst = ((rhs, base_hbm), (resid, resid_hbm))[phase]
        at = pl.multiple_of(side * size, LANES)
        return pltpu.make_async_copy(
            src.at[chunk, :, pl.ds(at, size)],
            dst.at[:, pl.ds(pl.multiple_of(chunk * size, LANES), size)],
            out_sem.at[phase, chunk],
        )

    sums[...] = jnp.zeros_like(sums)

    def first_low(chunk, value):
        rhs[chunk] = value
        return value

    def first_account(chunk):
        own = own_part(rhs, chunk)
        square = own * own
        sums[0] += fold(square)
        sums[1] += fold(square * own_part(lam, chunk))
        out_copy(0, chunk).start()

    product(0, first_low, first_account)

    first_row = lax.rem(me_f, owners) * per

    def weighted(value, other):
        out = jnp.zeros((rows, LANES), jnp.float32)
        for t in range(per):
            out = out + curvew[pl.ds(first_row + t, 1), :] * value[t] * other[t]
        return jnp.sum(out, axis=1, keepdims=True)

    mine = scattered(0)
    held[...] = mine
    for t in range(per):
        gathered[me_f, t] = (curvew[pl.ds(first_row + t, 1), :] * mine[t]).astype(jnp.bfloat16)
    whole_tang = launch(feat_copies(lambda peer: gathered.at[me_f], lambda k: gathered.at[me_f], 3))
    feat_packets[0, 0] = packed(
        [jnp.sum(sums[at], axis=1, keepdims=True) for at in range(2)] + [weighted(mine, mine)]
    )
    feat_sums = launch(feat_copies(lambda peer: feat_packets.at[0, 0], lambda k: feat_packets.at[0, k], 5))
    receive(whole_tang)
    for g in range(groups_n):
        left[:, g * LANES : (g + 1) * LANES] = gathered[g // per, g % per]
    receive(feat_sums)
    packet = feat_packets[0, 0]
    for k in range(1, nf):
        packet = packet + feat_packets[0, k]
    packets[0, 0] = packet
    shared = launch(ex_copies(lambda peer: packets.at[0, 0], lambda k: packets.at[0, k], 0))
    waiting.extend(shared)

    sums[...] = jnp.zeros_like(sums)
    grouped[...] = jnp.zeros_like(grouped)

    def second_low(chunk, value):
        @pl.when(chunk == 0)
        def _():
            for copy in shared:
                copy.wait_recv()
            packet = packets[0, 0]
            for k in range(1, ne):
                packet = packet + packets[0, k]
            norm, damp, along = packet[0:1], packet[1:2], packet[2:3]
            steps = norm / (along / total + damp)
            packets[3, 0] = jnp.concatenate([steps, packet[:7]], axis=0)
            alpha[...] = jnp.transpose(packets[3, 0])[:rows, 0:1]

        base = rhs[chunk]
        value = base - alpha[...] * (value / total + lam[chunk] * base)
        resid[chunk] = value
        return value

    def second_account(chunk):
        own = own_part(resid, chunk)
        before = own_part(rhs, chunk)
        scaled = own_part(lam, chunk) * own
        sums[0] += fold(own * own)
        sums[1] += fold(scaled * own)
        sums[2] += fold(scaled * before)
        at = pl.multiple_of(me_e * share + chunk * size, LANES)
        w = weight_row(at)
        pieces = jnp.concatenate(split_in(before * w, 2) + split_in(own * w, 2), axis=0)
        grouped[...] += lax.dot_general(
            one_hot(ids_ref[:, pl.ds(at, size)], blocks),
            pieces,
            (((1,), (1,)), ((), ())),
            preferred_element_type=jnp.float32,
        )
        out_copy(1, chunk).start()

    product(1, second_low, second_account)

    for f in range(nf):
        groups[f] = grouped[f * nb_feat : (f + 1) * nb_feat, :]
    sent = launch(feat_copies(lambda peer: groups.at[peer], lambda k: group_parts.at[k], 4))
    turned = scattered(1)
    packets[1, 0] = packed(
        [jnp.sum(sums[at], axis=1, keepdims=True) for at in range(3)]
        + [weighted(turned, turned), weighted(turned, held[...])]
    )
    ex_sums = launch(ex_copies(lambda peer: packets.at[1, 0], lambda k: packets.at[1, k], 1))
    receive(sent)
    owned = groups[me_f]
    for k in range(1, nf):
        owned = owned + group_parts[k]
    for e in range(ne):
        own_groups[e] = owned[e * nb_own : (e + 1) * nb_own, :]
    group_sums = launch(ex_copies(lambda peer: own_groups.at[peer], lambda k: own_parts.at[k], 2))
    receive(ex_sums)
    packet = packets[1, 0]
    for k in range(1, ne):
        packet = packet + packets[1, k]
    feat_packets[1, 0] = packet
    feat_sums = launch(feat_copies(lambda peer: feat_packets.at[1, 0], lambda k: feat_packets.at[1, k], 6))
    receive(group_sums)
    mine = own_groups[me_e]
    for k in range(1, ne):
        mine = mine + own_parts[k]
    first_block = (me_f * ne + me_e) * nb_own
    mine = -own_strengths[pl.ds(first_block, nb_own), 0:1] * mine
    receive(feat_sums)
    for k in range(1, nf):
        packet = packet + feat_packets[1, k]

    norm_next, damp_next, damp_cross, curved_next, curved_cross = (packet[at : at + 1, :rows] for at in range(5))
    before = packets[3, 0]
    alphas, norm, damp, along = (before[at : at + 1, :rows] for at in range(4))
    beta = norm_next / norm
    curved = curved_next + 2.0 * beta * curved_cross + beta * beta * along
    damped = damp_next + 2.0 * beta * damp_cross + beta * beta * damp
    step = norm_next / (curved / total + damped)
    first = alphas + step * beta
    coef_ref[0:1, :rows] = first
    coef_ref[1:2, :rows] = step
    hyper_ref[...] = first * (mine[:, :rows] + mine[:, rows : 2 * rows]) + step * (
        mine[:, 2 * rows : 3 * rows] + mine[:, 3 * rows : 4 * rows]
    )

    for copy in waiting:
        copy.wait_send()

    @pl.loop(0, chunks)
    def _(i):
        for phase in range(2):
            out_copy(phase, i).wait()
            for kind in range(3):
                pair_copy(phase, kind, i).wait_send()


def shards(examples, weights, labels, split, val_weight, strengths, block_ids):
    ne = lax.axis_size("ex")
    nf = lax.axis_size("feat")
    n, width = examples.shape
    rows = val_weight.shape[0]
    blocks = strengths.shape[0]
    share = width // ne
    size = LANES
    while size < 512 and share % (2 * size) == 0:
        size *= 2
    chunks = share // size
    slots = max(LAG_TANG + 2, RING_BYTES // (2 * n * ne * size))
    groups_n = n // LANES
    per = groups_n // min(nf, groups_n)
    nb_feat = blocks // nf
    nb_own = nb_feat // ne
    dims = (nf, ne, n, width, rows, blocks, share, size, chunks, slots)
    half = 2 * size
    f32, bf16 = jnp.float32, jnp.bfloat16
    base, resid, coef, hyper = pl.pallas_call(
        functools.partial(kernel, dims),
        out_shape=(
            jax.ShapeDtypeStruct((rows, share), f32),
            jax.ShapeDtypeStruct((rows, share), f32),
            jax.ShapeDtypeStruct((8, LANES), f32),
            jax.ShapeDtypeStruct((nb_own, rows), f32),
        ),
        in_specs=[ANY] + [VMEM] * 6,
        out_specs=(ANY, ANY, VMEM, VMEM),
        scratch_shapes=[
            pltpu.VMEM((slots, n, 2 * half), bf16),
            pltpu.VMEM((2 * half, n), bf16),
            pltpu.VMEM((width // LANES, LANES), f32),
            pltpu.VMEM((groups_n, LANES), f32),
            pltpu.VMEM((nf, groups_n, LANES), f32),
            pltpu.VMEM((chunks, 1, half), f32),
            pltpu.VMEM((groups_n, LANES), f32),
            pltpu.VMEM((rows, n), bf16),
            pltpu.VMEM((2, chunks, rows, half), bf16),
            pltpu.VMEM((2, chunks, rows, half), bf16),
            pltpu.VMEM((2, chunks, rows, half), bf16),
            pltpu.VMEM((2, chunks, rows, half), bf16),
            pltpu.VMEM((2, chunks, 2, rows, half), bf16),
            pltpu.VMEM((chunks, rows, half), f32),
            pltpu.VMEM((2, groups_n, rows, LANES), f32),
            pltpu.VMEM((2, nf, per, rows, LANES), f32),
            pltpu.VMEM((per, rows, LANES), f32),
            pltpu.VMEM((nf, per, rows, LANES), bf16),
            pltpu.VMEM((3, rows, LANES), f32),
            pltpu.VMEM((rows, 1), f32),
            pltpu.VMEM((4, ne, 8, LANES), f32),
            pltpu.VMEM((2, nf, 8, LANES), f32),
            pltpu.VMEM((blocks, 4 * rows), f32),
            pltpu.VMEM((nf, nb_feat, 4 * rows), f32),
            pltpu.VMEM((nf, nb_feat, 4 * rows), f32),
            pltpu.VMEM((ne, nb_own, 4 * rows), f32),
            pltpu.VMEM((ne, nb_own, 4 * rows), f32),
            pltpu.VMEM((blocks, 8), f32),
            pltpu.VMEM((chunks, rows, half), f32),
            pltpu.SemaphoreType.DMA((slots, 4)),
            pltpu.SemaphoreType.DMA((2, chunks)),
            pltpu.SemaphoreType.DMA((2, 3, 2, chunks)),
            pltpu.SemaphoreType.DMA((7, 2, nf)),
            pltpu.SemaphoreType.DMA((3, 2, ne)),
        ],
        compiler_params=pltpu.CompilerParams(
            collective_id=0, has_side_effects=True, vmem_limit_bytes=60 * 2**20
        ),
    )(
        examples,
        weights.reshape(width // LANES, LANES),
        block_ids.reshape(1, width),
        labels.reshape(groups_n, LANES),
        split.reshape(groups_n, LANES),
        val_weight,
        strengths.reshape(1, blocks),
    )
    solve = coef[0, :rows, None] * base + coef[1, :rows, None] * resid
    return (solve, hyper.T)


def solution(mesh):
    placed = (P("ex", "feat"), P("feat"), P("ex"), P("ex"), P(None, "ex"), P(), P("feat"))
    return jax.shard_map(
        shards,
        mesh=mesh,
        in_specs=placed,
        out_specs=(P(None, ("feat", "ex")), P(None, ("feat", "ex"))),
        check_vma=False,
    )
```

```python
import functools
import math

import jax
import jax.numpy as jnp
from jax import lax
from jax.experimental import pallas as pl
from jax.experimental.pallas import tpu as pltpu
from jax.sharding import PartitionSpec as P

MESH = pl.DeviceIdType.MESH
VMEM = pl.BlockSpec(memory_space=pltpu.VMEM)
ANY = pl.BlockSpec(memory_space=pl.ANY)
LANES = 128
LAG_SUM, LAG_LOW, LAG_TANG = 1, 4, 5
RING_BYTES = 32 * 2**20


def address(axis, pos):
    if axis == "feat":
        return (pos, lax.axis_index("ex"))
    return (lax.axis_index("feat"), pos)


def flip(pos, mask):
    return pos + mask * (1 - 2 * lax.rem(lax.div(pos, mask), 2))


def fold(x):
    total = x[:, :LANES]
    for at in range(LANES, x.shape[1], LANES):
        total = total + x[:, at : at + LANES]
    return total


def packed(columns):
    rows = columns[0].shape[0]
    lanes = lax.broadcasted_iota(jnp.int32, (rows, LANES), 1)
    out = jnp.zeros((rows, LANES), jnp.float32)
    for lane, column in enumerate(columns):
        out = jnp.where(lanes == lane, column, out)
    out = jnp.transpose(out)[:8]
    return jnp.concatenate([out, jnp.zeros((8, LANES - rows), jnp.float32)], axis=1)


def split_in(x, pieces):
    parts = []
    for _ in range(pieces):
        part = x.astype(jnp.bfloat16)
        parts.append(part)
        x = x - part.astype(jnp.float32)
    return parts


def one_hot(ids, blocks):
    rows = lax.broadcasted_iota(jnp.int32, (blocks, ids.shape[1]), 0)
    return (rows == ids).astype(jnp.float32).astype(jnp.bfloat16)


def kernel(
    dims,
    x_hbm,
    w_ref,
    ids_ref,
    labels_ref,
    split_ref,
    vw_ref,
    strengths_ref,
    base_hbm,
    resid_hbm,
    coef_ref,
    hyper_ref,
    ring,
    turned_x,
    weights,
    margin,
    margins,
    lam,
    curvew,
    left,
    out_a,
    in_a,
    out_b,
    in_b,
    low,
    rhs,
    tang,
    parts,
    held,
    gathered,
    sums,
    alpha,
    packets,
    feat_packets,
    grouped,
    groups,
    group_parts,
    own_groups,
    own_parts,
    own_strengths,
    resid,
    ring_sem,
    out_sem,
    pair_sem,
    feat_sem,
    ex_sem,
):
    nf, ne, n, width, rows, blocks, share, size, chunks, slots = dims
    total = n * ne
    groups_n = n // LANES
    owners = min(nf, groups_n)
    per = groups_n // owners
    nb_feat = blocks // nf
    nb_own = nb_feat // ne
    me_f = lax.axis_index("feat")
    me_e = lax.axis_index("ex")
    core = lax.rem(me_e, 2)
    side = lax.div(me_e, 2)
    half = 2 * size

    barrier = pltpu.get_barrier_semaphore()
    for axis, me, count in (("feat", me_f, nf), ("ex", me_e, ne)):
        for k in range(1, count):
            pl.semaphore_signal(
                barrier, inc=1, device_id=address(axis, lax.rem(me + k, count)), device_id_type=MESH
            )

    def load(turn):
        chunk = lax.rem(turn, chunks)
        slot = lax.rem(turn, slots)
        copies = []
        for h in range(2):
            for x in range(2):
                at = pl.multiple_of((h + 2 * x) * share + chunk * size, LANES)
                copies.append(
                    pltpu.make_async_copy(
                        x_hbm.at[:, pl.ds(at, size)],
                        ring.at[slot, :, pl.ds(h * half + x * size, size)],
                        ring_sem.at[slot, 2 * h + x],
                    )
                )
        return copies

    def begin(turn):
        for copy in load(turn):
            copy.start()

    def arrived(turn):
        for copy in load(turn):
            copy.wait()

    def refill(turn):
        @pl.when(turn + slots < 3 * chunks)
        def _():
            begin(turn + slots)

    for turn in range(min(slots, 3 * chunks)):
        begin(turn)

    def columns(ref, chunk, h, x):
        at = pl.multiple_of((h + 2 * x) * share + chunk * size, LANES)
        return ref[:, pl.ds(at, size)]

    levels = jnp.concatenate(
        split_in(strengths_ref[...], 3) + [jnp.zeros((5, blocks), jnp.bfloat16)], axis=0
    )
    own_strengths[...] = jnp.transpose(jnp.broadcast_to(strengths_ref[...], (8, blocks)))
    margin[...] = jnp.zeros_like(margin)
    weights[...] = w_ref[...].astype(jnp.float32)

    def weight_row(start):
        row = lax.div(start, LANES)
        return jnp.concatenate([weights[pl.ds(row + t, 1), :] for t in range(size // LANES)], axis=1)

    @pl.loop(0, chunks)
    def _(i):
        arrived(i)
        slot = lax.rem(i, slots)
        w = jnp.concatenate([weight_row((h + 2 * x) * share + i * size) for h in range(2) for x in range(2)], axis=1)
        part = lax.dot_general(
            w.astype(jnp.bfloat16), ring[slot], (((1,), (1,)), ((), ())), preferred_element_type=jnp.float32
        )
        for g in range(groups_n):
            margin[g : g + 1, :] += part[:, g * LANES : (g + 1) * LANES]
        refill(i)
        ids = jnp.concatenate([columns(ids_ref, i, core, x) for x in range(2)], axis=1)
        found = jnp.dot(levels, one_hot(ids, blocks), preferred_element_type=jnp.float32)
        lam[i] = found[0:1] + found[1:2] + found[2:3]

    pl.semaphore_wait(barrier, nf - 1 + ne - 1)

    def remote(src, dst, sems, axis, peer):
        return pltpu.make_async_remote_copy(
            src_ref=src,
            dst_ref=dst,
            send_sem=sems[0],
            recv_sem=sems[1],
            device_id=address(axis, peer),
            device_id_type=MESH,
        )

    def feat_copies(src, dst, kind):
        return [
            remote(src(lax.rem(me_f + k, nf)), dst(k), [feat_sem.at[kind, d, k] for d in range(2)], "feat", lax.rem(me_f + k, nf))
            for k in range(1, nf)
        ]

    def ex_copies(src, dst, kind):
        return [
            remote(src(lax.rem(me_e + k, ne)), dst(k), [ex_sem.at[kind, d, k] for d in range(2)], "ex", lax.rem(me_e + k, ne))
            for k in range(1, ne)
        ]

    def launch(copies):
        for copy in copies:
            copy.start()
        return copies

    waiting = []

    def settle():
        while waiting:
            waiting.pop().wait_send()

    def receive(copies):
        for copy in copies:
            copy.wait_recv()
        waiting.extend(copies)

    receive(launch(feat_copies(lambda peer: margin, lambda k: margins.at[k], 0)))
    whole = margin[...]
    for k in range(1, nf):
        whole = whole + margins[k]
    prob = 1.0 / (1.0 + jnp.exp(-whole))
    train = split_ref[...].astype(jnp.float32)
    curvew[...] = train * prob * (1.0 - prob)
    err = (1.0 - train) * (prob - labels_ref[...].astype(jnp.float32))
    root = jnp.float32(math.sqrt(total))
    for g in range(groups_n):
        at = slice(g * LANES, (g + 1) * LANES)
        left[:, at] = (vw_ref[:, at] * err[g : g + 1] / root).astype(jnp.bfloat16)

    def pair_copy(phase, kind, chunk):
        src, dst, mask = (
            (out_a.at[phase, chunk], in_a.at[phase, chunk], 1),
            (out_b.at[phase, chunk], in_b.at[phase, chunk], 2),
            (low.at[phase, chunk, core], low.at[phase, chunk, core], 1),
        )[kind]
        return remote(src, dst, [pair_sem.at[phase, kind, d, chunk] for d in range(2)], "ex", flip(me_e, mask))

    def product(phase, finish, account):
        tang[phase] = jnp.zeros_like(tang[phase])
        base = (phase + 1) * chunks
        keep = (rhs, resid)[phase]

        def low_step(i):
            chunk = i - LAG_LOW
            pair_copy(phase, 1, chunk).wait_recv()
            value = finish(chunk, keep[chunk] + in_b[phase, chunk].astype(jnp.float32))
            low[phase, chunk, core] = value.astype(jnp.bfloat16)
            pair_copy(phase, 2, chunk).start()

        def sum_step(i):
            chunk = i - LAG_SUM
            pair_copy(phase, 0, chunk).wait_recv()
            value = keep[chunk] + in_a[phase, chunk].astype(jnp.float32)
            keep[chunk] = value
            out_b[phase, chunk] = value.astype(jnp.bfloat16)
            pair_copy(phase, 1, chunk).start()

        def matmuls(i, first, second):
            if first:
                arrived(base + i)
                slot = lax.rem(base + i, slots)
                away = ring[slot, :, pl.ds(pl.multiple_of((1 - core) * half, LANES), half)]
                out_a[phase, i] = jnp.dot(left[...], away, preferred_element_type=jnp.float32).astype(jnp.bfloat16)
                pair_copy(phase, 0, i).start()
            if second:
                chunk = i - LAG_TANG
                held_slot = lax.rem(base + chunk, slots)
                pair_copy(phase, 2, chunk).wait_recv()
                account(chunk)
                if first:
                    turned_x[...] = jnp.transpose(ring[held_slot])
                else:
                    turned_x[:half] = jnp.transpose(ring[held_slot, :, :half])
            if first:
                mine = ring[slot, :, pl.ds(pl.multiple_of(core * half, LANES), half)]
                keep[i] = jnp.dot(left[...], mine, preferred_element_type=jnp.float32)
            if second and first:
                direc = jnp.concatenate([low[phase, chunk, 0], low[phase, chunk, 1]], axis=1)
                part = jnp.dot(direc, turned_x[...], preferred_element_type=jnp.float32)
            elif second:
                part = jnp.dot(low[phase, chunk, 0], turned_x[:half], preferred_element_type=jnp.float32)
                part = part + lax.dot_general(
                    low[phase, chunk, 1],
                    ring[held_slot, :, half:],
                    (((1,), (1,)), ((), ())),
                    preferred_element_type=jnp.float32,
                )
            if second:
                for g in range(groups_n):
                    tang[phase, g] += part[:, g * LANES : (g + 1) * LANES]
                refill(base + chunk)

        ramp = min(LAG_TANG, chunks)

        @pl.loop(0, ramp)
        def _(i):
            pl.when((i >= LAG_LOW) & (i < chunks + LAG_LOW))(lambda: low_step(i))
            pl.when((i >= LAG_SUM) & (i < chunks + LAG_SUM))(lambda: sum_step(i))
            matmuls(i, True, False)

        @pl.loop(ramp, chunks)
        def _(i):
            low_step(i)
            sum_step(i)
            matmuls(i, True, True)

        @pl.loop(chunks, chunks + LAG_TANG)
        def _(i):
            pl.when((i >= LAG_LOW) & (i < chunks + LAG_LOW))(lambda: low_step(i))
            pl.when((i >= LAG_SUM) & (i < chunks + LAG_SUM))(lambda: sum_step(i))
            pl.when(i >= LAG_TANG)(lambda: matmuls(i, False, True))

    def settle_product(phase):
        @pl.loop(0, chunks)
        def _(i):
            out_copy(phase, i).wait()
            for kind in range(3):
                pair_copy(phase, kind, i).wait_send()

    def scattered(phase, meanwhile):
        peers = [lax.rem(me_f + k, nf) for k in range(1, nf)]
        copies = feat_copies(
            lambda peer: tang.at[phase, pl.ds(lax.rem(peer, owners) * per, per)], lambda k: parts.at[phase, k], 1 + phase
        )
        if owners == nf:
            launch(copies)
            sent = meanwhile()
            settle()
            receive(copies)
        else:
            for peer, copy in zip(peers, copies):
                pl.when(peer < owners)(copy.start)
            sent = meanwhile()
            settle()

            @pl.when(me_f < owners)
            def _():
                for copy in copies:
                    copy.wait_recv()

            for peer, copy in zip(peers, copies):
                pl.when(peer < owners)(copy.wait_send)
        value = tang[phase, pl.ds(lax.rem(me_f, owners) * per, per)]
        for k in range(1, nf):
            value = value + parts[phase, k]
        if owners == nf:
            return value, sent
        return jnp.where(me_f < owners, value, 0.0), sent

    def own_part(ref, chunk):
        return ref[chunk, :, pl.ds(pl.multiple_of(side * size, LANES), size)]

    def out_copy(phase, chunk):
        src, dst = ((rhs, base_hbm), (resid, resid_hbm))[phase]
        at = pl.multiple_of(side * size, LANES)
        return pltpu.make_async_copy(
            src.at[chunk, :, pl.ds(at, size)],
            dst.at[:, pl.ds(pl.multiple_of(chunk * size, LANES), size)],
            out_sem.at[phase, chunk],
        )

    sums[...] = jnp.zeros_like(sums)

    def first_low(chunk, value):
        rhs[chunk] = value
        return value

    def first_account(chunk):
        own = own_part(rhs, chunk)
        square = own * own
        sums[0] += fold(square)
        sums[1] += fold(square * own_part(lam, chunk))
        out_copy(0, chunk).start()

    product(0, first_low, first_account)

    first_row = lax.rem(me_f, owners) * per

    def weighted(value, other):
        out = jnp.zeros((rows, LANES), jnp.float32)
        for t in range(per):
            out = out + curvew[pl.ds(first_row + t, 1), :] * value[t] * other[t]
        return jnp.sum(out, axis=1, keepdims=True)

    mine, _ = scattered(0, lambda: settle_product(0))
    held[...] = mine
    for t in range(per):
        gathered[me_f, t] = (curvew[pl.ds(first_row + t, 1), :] * mine[t]).astype(jnp.bfloat16)
    whole_tang = launch(feat_copies(lambda peer: gathered.at[me_f], lambda k: gathered.at[me_f], 3))
    feat_packets[0, 0] = packed(
        [jnp.sum(sums[at], axis=1, keepdims=True) for at in range(2)] + [weighted(mine, mine)]
    )
    feat_sums = launch(feat_copies(lambda peer: feat_packets.at[0, 0], lambda k: feat_packets.at[0, k], 5))
    receive(whole_tang)
    for g in range(groups_n):
        left[:, g * LANES : (g + 1) * LANES] = gathered[g // per, g % per]
    receive(feat_sums)
    packet = feat_packets[0, 0]
    for k in range(1, nf):
        packet = packet + feat_packets[0, k]
    packets[0, 0] = packet
    shared = launch(ex_copies(lambda peer: packets.at[0, 0], lambda k: packets.at[0, k], 0))
    waiting.extend(shared)

    sums[...] = jnp.zeros_like(sums)
    grouped[...] = jnp.zeros_like(grouped)

    def second_low(chunk, value):
        @pl.when(chunk == 0)
        def _():
            for copy in shared:
                copy.wait_recv()
            packet = packets[0, 0]
            for k in range(1, ne):
                packet = packet + packets[0, k]
            norm, damp, along = packet[0:1], packet[1:2], packet[2:3]
            steps = norm / (along / total + damp)
            packets[3, 0] = jnp.concatenate([steps, packet[:7]], axis=0)
            alpha[...] = jnp.transpose(packets[3, 0])[:rows, 0:1]

        base = rhs[chunk]
        value = base - alpha[...] * (value / total + lam[chunk] * base)
        resid[chunk] = value
        return value

    def second_account(chunk):
        own = own_part(resid, chunk)
        before = own_part(rhs, chunk)
        scaled = own_part(lam, chunk) * own
        sums[0] += fold(own * own)
        sums[1] += fold(scaled * own)
        sums[2] += fold(scaled * before)
        at = pl.multiple_of(me_e * share + chunk * size, LANES)
        w = weight_row(at)
        pieces = jnp.concatenate(split_in(before * w, 2) + split_in(own * w, 2), axis=0)
        grouped[...] += lax.dot_general(
            one_hot(ids_ref[:, pl.ds(at, size)], blocks),
            pieces,
            (((1,), (1,)), ((), ())),
            preferred_element_type=jnp.float32,
        )
        out_copy(1, chunk).start()

    product(1, second_low, second_account)

    def send_groups():
        for f in range(nf):
            groups[f] = grouped[f * nb_feat : (f + 1) * nb_feat, :]
        sent = launch(feat_copies(lambda peer: groups.at[peer], lambda k: group_parts.at[k], 4))
        settle_product(1)
        return sent

    turned, sent = scattered(1, send_groups)
    packets[1, 0] = packed(
        [jnp.sum(sums[at], axis=1, keepdims=True) for at in range(3)]
        + [weighted(turned, turned), weighted(turned, held[...])]
    )
    ex_sums = launch(ex_copies(lambda peer: packets.at[1, 0], lambda k: packets.at[1, k], 1))
    receive(sent)
    owned = groups[me_f]
    for k in range(1, nf):
        owned = owned + group_parts[k]
    for e in range(ne):
        own_groups[e] = owned[e * nb_own : (e + 1) * nb_own, :]
    group_sums = launch(ex_copies(lambda peer: own_groups.at[peer], lambda k: own_parts.at[k], 2))
    receive(ex_sums)
    packet = packets[1, 0]
    for k in range(1, ne):
        packet = packet + packets[1, k]
    feat_packets[1, 0] = packet
    feat_sums = launch(feat_copies(lambda peer: feat_packets.at[1, 0], lambda k: feat_packets.at[1, k], 6))
    receive(group_sums)
    mine = own_groups[me_e]
    for k in range(1, ne):
        mine = mine + own_parts[k]
    first_block = (me_f * ne + me_e) * nb_own
    mine = -own_strengths[pl.ds(first_block, nb_own), 0:1] * mine
    settle()
    receive(feat_sums)
    for k in range(1, nf):
        packet = packet + feat_packets[1, k]

    norm_next, damp_next, damp_cross, curved_next, curved_cross = (packet[at : at + 1, :rows] for at in range(5))
    before = packets[3, 0]
    alphas, norm, damp, along = (before[at : at + 1, :rows] for at in range(4))
    beta = norm_next / norm
    curved = curved_next + 2.0 * beta * curved_cross + beta * beta * along
    damped = damp_next + 2.0 * beta * damp_cross + beta * beta * damp
    step = norm_next / (curved / total + damped)
    first = alphas + step * beta
    coef_ref[...] = jnp.concatenate(
        [jnp.broadcast_to(x, (4, rows)) for x in (first, step)], axis=0
    )
    hyper_ref[...] = first * (mine[:, :rows] + mine[:, rows : 2 * rows]) + step * (
        mine[:, 2 * rows : 3 * rows] + mine[:, 3 * rows : 4 * rows]
    )

    settle()


def combine(base_ref, resid_ref, coef_ref, blocks_ref, solve_ref, hyper_ref):
    columns = jnp.transpose(coef_ref[...])
    solve_ref[...] = columns[:, 0:1] * base_ref[...] + columns[:, 4:5] * resid_ref[...]
    hyper_ref[...] = blocks_ref[...]


def shards(examples, weights, labels, split, val_weight, strengths, block_ids):
    ne = lax.axis_size("ex")
    nf = lax.axis_size("feat")
    n, width = examples.shape
    rows = val_weight.shape[0]
    blocks = strengths.shape[0]
    share = width // ne
    size = LANES
    while size < 512 and share % (2 * size) == 0:
        size *= 2
    chunks = share // size
    slots = max(LAG_TANG + 2, RING_BYTES // (2 * n * ne * size))
    groups_n = n // LANES
    per = groups_n // min(nf, groups_n)
    nb_feat = blocks // nf
    nb_own = nb_feat // ne
    dims = (nf, ne, n, width, rows, blocks, share, size, chunks, slots)
    half = 2 * size
    f32, bf16 = jnp.float32, jnp.bfloat16
    base, resid, coef, hyper = pl.pallas_call(
        functools.partial(kernel, dims),
        out_shape=(
            jax.ShapeDtypeStruct((rows, share), f32),
            jax.ShapeDtypeStruct((rows, share), f32),
            jax.ShapeDtypeStruct((8, rows), f32),
            jax.ShapeDtypeStruct((nb_own, rows), f32),
        ),
        in_specs=[ANY] + [VMEM] * 6,
        out_specs=(ANY, ANY, VMEM, VMEM),
        scratch_shapes=[
            pltpu.VMEM((slots, n, 2 * half), bf16),
            pltpu.VMEM((2 * half, n), bf16),
            pltpu.VMEM((width // LANES, LANES), f32),
            pltpu.VMEM((groups_n, LANES), f32),
            pltpu.VMEM((nf, groups_n, LANES), f32),
            pltpu.VMEM((chunks, 1, half), f32),
            pltpu.VMEM((groups_n, LANES), f32),
            pltpu.VMEM((rows, n), bf16),
            pltpu.VMEM((2, chunks, rows, half), bf16),
            pltpu.VMEM((2, chunks, rows, half), bf16),
            pltpu.VMEM((2, chunks, rows, half), bf16),
            pltpu.VMEM((2, chunks, rows, half), bf16),
            pltpu.VMEM((2, chunks, 2, rows, half), bf16),
            pltpu.VMEM((chunks, rows, half), f32),
            pltpu.VMEM((2, groups_n, rows, LANES), f32),
            pltpu.VMEM((2, nf, per, rows, LANES), f32),
            pltpu.VMEM((per, rows, LANES), f32),
            pltpu.VMEM((nf, per, rows, LANES), bf16),
            pltpu.VMEM((3, rows, LANES), f32),
            pltpu.VMEM((rows, 1), f32),
            pltpu.VMEM((4, ne, 8, LANES), f32),
            pltpu.VMEM((2, nf, 8, LANES), f32),
            pltpu.VMEM((blocks, 4 * rows), f32),
            pltpu.VMEM((nf, nb_feat, 4 * rows), f32),
            pltpu.VMEM((nf, nb_feat, 4 * rows), f32),
            pltpu.VMEM((ne, nb_own, 4 * rows), f32),
            pltpu.VMEM((ne, nb_own, 4 * rows), f32),
            pltpu.VMEM((blocks, 8), f32),
            pltpu.VMEM((chunks, rows, half), f32),
            pltpu.SemaphoreType.DMA((slots, 4)),
            pltpu.SemaphoreType.DMA((2, chunks)),
            pltpu.SemaphoreType.DMA((2, 3, 2, chunks)),
            pltpu.SemaphoreType.DMA((7, 2, nf)),
            pltpu.SemaphoreType.DMA((3, 2, ne)),
        ],
        compiler_params=pltpu.CompilerParams(
            collective_id=0, has_side_effects=True, vmem_limit_bytes=60 * 2**20
        ),
    )(
        examples,
        weights.reshape(width // LANES, LANES),
        block_ids.reshape(1, width),
        labels.reshape(groups_n, LANES),
        split.reshape(groups_n, LANES),
        val_weight,
        strengths.reshape(1, blocks),
    )
    block = pl.BlockSpec((rows, share // 4), lambda i: (0, i))
    same = lambda like: pl.BlockSpec(like.shape, lambda i: (0, 0))
    solve, hyper = pl.pallas_call(
        combine,
        grid=(4,),
        out_shape=(jax.ShapeDtypeStruct(base.shape, f32), jax.ShapeDtypeStruct(hyper.shape, f32)),
        in_specs=[block, block, same(coef), same(hyper)],
        out_specs=(block, same(hyper)),
    )(base, resid, coef, hyper)
    return (solve, hyper.T)


def solution(mesh):
    placed = (P("ex", "feat"), P("feat"), P("ex"), P("ex"), P(None, "ex"), P(), P("feat"))
    return jax.shard_map(
        shards,
        mesh=mesh,
        in_specs=placed,
        out_specs=(P(None, ("feat", "ex")), P(None, ("feat", "ex"))),
        check_vma=False,
    )
```
